32 devices in a mesh: tile: 8 (over z, x), section: 4 (over y, core).
Axes of the slice: x: 2, y: 2, z: 4, core: 2. Of those that a mesh axis runs over, the one named last changes fastest.
Arguments:
- states: bfloat16 [2, 192, 8, 8, 256], P(None, 'tile'), may hold values from -6 to 6
- conv_weight: bfloat16 [4, 2, 3, 3, 256, 256], P('section'), may hold values from -0.1875 to 0.1875
- skip_weight: bfloat16 [4, 256, 256], P('section'), may hold values from -0.375 to 0.375
- bias: bfloat16 [4, 2, 256], P('section'), may hold values from -3 to 3
- placement: int32 [8], replicated, may hold values from 0 to 7, each once
Outputs:
- activations: bfloat16 [4, 2, 192, 8, 8, 256], P('section', None, 'tile')
The draws below stay inside these ranges and needn't reach their ends.
Inputs may be any that keep to these rules, and one draw needn't show every extreme that they name: placement is a permutation of 0 .. 7.
All inputs are finite; a program needn't handle non-finite values.
Results may differ from the reference program's by a relative error of at most 0.017.
Values may be sent and summed in bfloat16 or wider, within the bound.
A program may use at most 64 MiB of HBM per device.

```python
import jax
import jax.numpy as jnp
import numpy as np
from jax import lax

C = 256
LAYERS = 2
MB = 2
PR = 4
TILE = 8
PATCHES = 192
BLOCKS = 8
SECTIONS = 4


def steps_of(own_key, dims, cuts, smallest, high):
    def one(dim, shards_of):
        heights = jax.random.uniform(jax.random.fold_in(jax.random.fold_in(own_key, 6), dim), (shards_of,), jnp.float32, smallest / len(cuts), high / len(cuts))
        return jnp.repeat(jnp.exp(heights), dims[dim] // shards_of).reshape((-1,) + (1,) * (len(dims) - dim - 1))

    loudness = one(*cuts[0])
    for cut in cuts[1:]:
        loudness = loudness * one(*cut)
    return loudness


def normal_values(key, dims, spread, bound, cuts=(), held_as=jnp.bfloat16):
    values = jax.random.normal(key, dims, jnp.float32) * spread
    if len(cuts) > 0:
        values = steps_of(key, dims, cuts, -0.22, 0.18) * values
    return jnp.clip(values, min=-bound, max=bound).astype(held_as)


def setup_inputs(seed: int = 0) -> dict:
    key_list = jax.random.split(jax.random.key(seed), 6)
    states = normal_values(key_list[0], (MB, PATCHES, TILE, TILE, C), 1.0, 6.0, ((1, 8),))
    conv_weight = normal_values(key_list[1], (SECTIONS, LAYERS, 3, 3, C, C), (9 * C // 2) ** -0.5, 0.1875, ((0, 4),))
    skip_weight = normal_values(key_list[2], (SECTIONS, C, C), C ** -0.5, 0.375, ((0, 4),))
    bias = normal_values(key_list[3], (SECTIONS, LAYERS, C), 0.5, 3.0, ((0, 4),))
    placement = jax.random.permutation(key_list[4], BLOCKS).astype(jnp.int32)
    return dict(states=states, conv_weight=conv_weight, skip_weight=skip_weight, bias=bias, placement=placement)


def face_across(face_num, direction):
    cycle = face_num // 4
    column = face_num % 4
    if cycle == 0:
        table = [4 + column, 4 + (column + 1) % 4, (column + 1) % 4, (column + 3) % 4]
    elif cycle == 1:
        table = [8 + (column + 3) % 4, 8 + column, column, (column + 3) % 4]
    else:
        table = [8 + (column + 3) % 4, 8 + (column + 1) % 4, 4 + (column + 1) % 4, 4 + column]
    return table[direction]


def locate(face_num, coord_x, coord_y, face_span):
    if 0 <= coord_x < face_span and 0 <= coord_y < face_span:
        return face_num, coord_x, coord_y
    if coord_x < 0:
        direction = 0
    elif coord_y < 0:
        direction = 1
    elif coord_x >= face_span:
        direction = 2
    else:
        direction = 3
    cycle = face_num // 4
    target = face_across(face_num, direction)
    coord_x = coord_x % face_span
    coord_y = coord_y % face_span
    if (cycle == 0 and direction == 2) or (cycle == 2 and direction == 0):
        coord_x, coord_y = coord_y, face_span - 1 - coord_x
    elif (cycle == 0 and direction == 3) or (cycle == 2 and direction == 1):
        coord_x, coord_y = face_span - 1 - coord_y, coord_x
    return target, coord_x, coord_y


def seam_tables(tiles):
    cell_side = 2
    face_span = tiles * cell_side
    face_tiles = tiles * tiles
    total = 12 * face_tiles
    neighbour = np.zeros((total, 4), np.int32)
    rim_side = np.zeros((total, 4), np.int32)
    flip_flag = np.zeros((total, 4), np.int32)
    for patch_num in range(total):
        cycle = patch_num % 3
        rest = patch_num // 3
        column = rest // face_tiles
        tile_y = (rest % face_tiles) // tiles
        tile_x = rest % tiles
        face_num = 4 * cycle + column
        base_x = tile_x * cell_side
        base_y = tile_y * cell_side
        for side_num in range(4):
            found = []
            for step_num in range(2):
                if side_num == 0:
                    point = (base_x - 1, base_y + step_num)
                elif side_num == 1:
                    point = (base_x + cell_side, base_y + step_num)
                elif side_num == 2:
                    point = (base_x + step_num, base_y - 1)
                else:
                    point = (base_x + step_num, base_y + cell_side)
                found.append(locate(face_num, point[0], point[1], face_span))
            face_a, first_x, first_y = found[0]
            face_b, second_x, second_y = found[1]
            neighbour[patch_num, side_num] = 3 * ((face_a % 4) * face_tiles + (first_y // cell_side) * tiles + first_x // cell_side) + face_a // 4
            if first_x == second_x:
                rim_side[patch_num, side_num] = 0 if first_x % cell_side == 0 else 1
                flip_flag[patch_num, side_num] = 1 if second_y < first_y else 0
            else:
                rim_side[patch_num, side_num] = 2 if first_y % cell_side == 0 else 3
                flip_flag[patch_num, side_num] = 1 if second_x < first_x else 0
    return neighbour, rim_side, flip_flag


def side_rims(fields):
    return jnp.stack([fields[:, :, 0], fields[:, :, -1], fields[:, 0], fields[:, -1]], axis=1)


def seam_padded(fields, neighbour, rim_side, flip_flag):
    rim_stack = side_rims(fields)
    padded = jnp.pad(fields, ((0, 0), (1, 1), (1, 1), (0, 0)))
    for side_num in range(4):
        strips = rim_stack[jnp.asarray(neighbour[:, side_num]), jnp.asarray(rim_side[:, side_num])]
        flipped = jnp.asarray(flip_flag[:, side_num] == 1)
        strips = jnp.where(flipped[:, None, None], strips[:, ::-1], strips)
        if side_num == 0:
            padded = padded.at[:, 1:-1, 0].set(strips)
        elif side_num == 1:
            padded = padded.at[:, 1:-1, -1].set(strips)
        elif side_num == 2:
            padded = padded.at[:, 0, 1:-1].set(strips)
        else:
            padded = padded.at[:, -1, 1:-1].set(strips)
    return padded


def section_apply(inputs, skip_in, conv_w, skip_w, biases, tables):
    hidden = inputs
    for layer_num in range(LAYERS):
        summed = lax.conv_general_dilated(
            seam_padded(hidden, tables[0], tables[1], tables[2]).astype(jnp.float32),
            conv_w[layer_num].astype(jnp.float32),
            (1, 1), "VALID",
            dimension_numbers=("NHWC", "HWIO", "NHWC"),
            precision=lax.Precision.HIGHEST)
        if layer_num == 0:
            summed = summed + jnp.einsum("pijc,cd->pijd", skip_in.astype(jnp.float32), skip_w.astype(jnp.float32), precision=lax.Precision.HIGHEST)
        summed = summed + biases[layer_num].astype(jnp.float32)
        hidden = jax.nn.gelu(summed, approximate=False).astype(jnp.bfloat16)
    return hidden


def reference(states, conv_weight, skip_weight, bias, placement):
    tables = seam_tables(PR)
    half_sections = SECTIONS // 2
    block_len = PATCHES // BLOCKS
    patch_of_row = (placement[:, None].astype(jnp.int32) * block_len + jnp.arange(block_len, dtype=jnp.int32)[None, :]).reshape(-1)
    natural = jnp.zeros_like(states).at[:, patch_of_row].set(states)
    per_batch = []
    for mb_num in range(MB):
        window_in = natural[mb_num]
        outputs = []
        hidden = window_in
        for section_num in range(SECTIONS):
            skip_in = window_in if section_num < half_sections else outputs[section_num - half_sections]
            hidden = section_apply(hidden, skip_in, conv_weight[section_num], skip_weight[section_num], bias[section_num], tables)
            outputs.append(hidden)
        per_batch.append(jnp.stack(outputs))
    result = jnp.stack(per_batch, axis=1)
    return result[:, :, patch_of_row]
```

```python
import functools

import jax
import jax.numpy as jnp
import numpy as np
from jax import lax
from jax.experimental import pallas as pl
from jax.experimental.pallas import tpu as pltpu
from jax.sharding import PartitionSpec as P

LAYERS = 2
PR = 4


def face_across(face_num, direction):
    cycle = face_num // 4
    column = face_num % 4
    if cycle == 0:
        table = [4 + column, 4 + (column + 1) % 4, (column + 1) % 4, (column + 3) % 4]
    elif cycle == 1:
        table = [8 + (column + 3) % 4, 8 + column, column, (column + 3) % 4]
    else:
        table = [8 + (column + 3) % 4, 8 + (column + 1) % 4, 4 + (column + 1) % 4, 4 + column]
    return table[direction]


def locate(face_num, coord_x, coord_y, face_span):
    if 0 <= coord_x < face_span and 0 <= coord_y < face_span:
        return (face_num, coord_x, coord_y)
    if coord_x < 0:
        direction = 0
    elif coord_y < 0:
        direction = 1
    elif coord_x >= face_span:
        direction = 2
    else:
        direction = 3
    cycle = face_num // 4
    target = face_across(face_num, direction)
    coord_x = coord_x % face_span
    coord_y = coord_y % face_span
    if cycle == 0 and direction == 2 or (cycle == 2 and direction == 0):
        coord_x, coord_y = (coord_y, face_span - 1 - coord_x)
    elif cycle == 0 and direction == 3 or (cycle == 2 and direction == 1):
        coord_x, coord_y = (face_span - 1 - coord_y, coord_x)
    return (target, coord_x, coord_y)


def seam_tables(tiles):
    cell_side = 2
    face_span = tiles * cell_side
    face_tiles = tiles * tiles
    total = 12 * face_tiles
    neighbour = np.zeros((total, 4), np.int32)
    rim_side = np.zeros((total, 4), np.int32)
    flip_flag = np.zeros((total, 4), np.int32)
    for patch_num in range(total):
        cycle = patch_num % 3
        rest = patch_num // 3
        column = rest // face_tiles
        tile_y = rest % face_tiles // tiles
        tile_x = rest % tiles
        face_num = 4 * cycle + column
        base_x = tile_x * cell_side
        base_y = tile_y * cell_side
        for side_num in range(4):
            found = []
            for step_num in range(2):
                if side_num == 0:
                    point = (base_x - 1, base_y + step_num)
                elif side_num == 1:
                    point = (base_x + cell_side, base_y + step_num)
                elif side_num == 2:
                    point = (base_x + step_num, base_y - 1)
                else:
                    point = (base_x + step_num, base_y + cell_side)
                found.append(locate(face_num, point[0], point[1], face_span))
            face_a, first_x, first_y = found[0]
            face_b, second_x, second_y = found[1]
            neighbour[patch_num, side_num] = (
                3 * (face_a % 4 * face_tiles + first_y // cell_side * tiles + first_x // cell_side)
                + face_a // 4
            )
            if first_x == second_x:
                rim_side[patch_num, side_num] = 0 if first_x % cell_side == 0 else 1
                flip_flag[patch_num, side_num] = 1 if second_y < first_y else 0
            else:
                rim_side[patch_num, side_num] = 2 if first_y % cell_side == 0 else 3
                flip_flag[patch_num, side_num] = 1 if second_x < first_x else 0
    return (neighbour, rim_side, flip_flag)


def off_device_routes(neighbour, rim_side, flip_flag, tile_count, per_dev):
    source_dev = (neighbour // per_dev).reshape(-1)
    dest_dev = np.repeat(np.arange(neighbour.shape[0]) // per_dev, 4)
    row = (neighbour % per_dev * 4 + rim_side).reshape(-1)
    away = source_dev != dest_dev
    slot_num = np.zeros(row.shape[0], np.int64)
    counts = np.zeros((tile_count, tile_count), np.int64)
    for e in np.flatnonzero(away):
        slot_num[e] = counts[source_dev[e], dest_dev[e]]
        counts[source_dev[e], dest_dev[e]] += 1
    send_row = np.zeros((tile_count, tile_count, int(counts.max())), np.int32)
    send_row[source_dev[away], dest_dev[away], slot_num[away]] = row[away]
    place = np.where(away, slot_num, row)
    recv_dev = source_dev.reshape(tile_count, per_dev, 4).astype(np.int32)
    recv_slot = place.reshape(tile_count, per_dev, 4).astype(np.int32)
    return (send_row, None, recv_dev, recv_slot)


MESH = pl.DeviceIdType.MESH
LANES = 128


def joined(ref, span):
    return jnp.concatenate([ref[b, span, :] for b in range(ref.shape[0])], axis=1)


def split_store(ref, span, value):
    for b in range(ref.shape[0]):
        ref[b, span, :] = value[:, b * LANES:(b + 1) * LANES]


def window_kernel(
    tiles, sections, patches, micro, slots,
    send_rows, recv_self, recv_from, recv_row,
    states, weights, skip_w, biases,
    out,
    chain_in, skip_in, hidden, left, right, padded, edge_low, edge_high, rims,
    outgoing, received_a, received_b,
    halo_send, halo_recv, move_send, move_recv,
):
    tile = lax.axis_index("tile")
    section = lax.axis_index("section")
    half = sections // 2
    side = states.shape[1]
    rows = states.shape[2]
    chan = states.shape[3]
    received = (received_a, received_b)

    def tile_at(by):
        return lax.rem(tile + by, tiles)

    barrier = pltpu.get_barrier_semaphore()
    for by in range(1, tiles):
        pl.semaphore_signal(barrier, inc=1, device_id={"tile": tile_at(by)}, device_id_type=MESH)
    for by in range(1, sections):
        pl.semaphore_signal(
            barrier, inc=1, device_id={"section": lax.rem(section + by, sections)}, device_id_type=MESH
        )
    pl.semaphore_wait(barrier, tiles - 1 + sections - 1)

    @pl.when(section == 0)
    def _():
        chain_in[...] = states[...]

    @pl.when(section < half)
    def _():
        skip_in[...] = states[...]

    column = lax.broadcasted_iota(jnp.int32, (rows // 8, 8, chan), 1)
    first = column == 0
    last = column == 7

    def halo_copy(layer, by):
        return pltpu.make_async_remote_copy(
            src_ref=outgoing.at[layer, by - 1],
            dst_ref=received[layer].at[by - 1],
            send_sem=halo_send.at[layer, by - 1],
            recv_sem=halo_recv.at[layer, by - 1],
            device_id={"tile": tile_at(by)},
            device_id_type=MESH,
        )

    def chain_copy(m):
        return pltpu.make_async_remote_copy(
            src_ref=out.at[m], dst_ref=chain_in.at[m],
            send_sem=move_send.at[0, m], recv_sem=move_recv.at[0, m],
            device_id={"section": lax.rem(section + 1, sections)}, device_id_type=MESH,
        )

    def skip_copy(m):
        return pltpu.make_async_remote_copy(
            src_ref=out.at[m], dst_ref=skip_in.at[m],
            send_sem=move_send.at[1, m], recv_sem=move_recv.at[1, m],
            device_id={"section": lax.rem(section + half, sections)}, device_id_type=MESH,
        )

    def run_layer(m, layer):
        for p in range(patches):
            top = (side - 1) * rows + p * 8
            for b in range(chan // LANES):
                lanes = slice(b * LANES, (b + 1) * LANES)
                rims[4 * p, :, lanes] = hidden[b, pl.ds(p * 8, 8, stride=rows), :]
                rims[4 * p + 1, :, lanes] = hidden[b, pl.ds(p * 8 + 7, 8, stride=rows), :]
                rims[4 * p + 2, :, lanes] = hidden[b, p * 8:p * 8 + 8, :]
                rims[4 * p + 3, :, lanes] = hidden[b, top:top + 8, :]
        for by in range(1, tiles):
            for q in range(slots):
                outgoing[layer, by - 1, q] = rims[send_rows[by * slots + q]].astype(jnp.bfloat16)
            halo_copy(layer, by).start()
        for r in range(side):
            padded[r + 1, :, chan:2 * chan] = joined(hidden, slice(r * rows, (r + 1) * rows)).astype(jnp.bfloat16)
        for by in range(1, tiles):
            halo_copy(layer, by).wait_recv()
        for p in range(patches):
            for k in range(4):
                e = 4 * p + k
                strip = jnp.where(
                    recv_self[e] == 1,
                    rims[recv_row[e]],
                    received[layer][recv_from[e], lax.rem(recv_row[e], slots)].astype(jnp.float32),
                )
                if k == 0:
                    for b in range(chan // LANES):
                        left[b, pl.ds(p * 8, 8, stride=rows), :] = strip[:, b * LANES:(b + 1) * LANES]
                elif k == 1:
                    for b in range(chan // LANES):
                        right[b, pl.ds(p * 8 + 7, 8, stride=rows), :] = strip[:, b * LANES:(b + 1) * LANES]
                elif k == 2:
                    edge_low[p * 8:p * 8 + 8, :] = strip
                else:
                    edge_high[p * 8:p * 8 + 8, :] = strip
        for r in range(side + 2):
            if r == 0 or r == side + 1:
                values = (edge_low if r == 0 else edge_high)[...].reshape(rows // 8, 8, chan)
                before = jnp.zeros_like(values)
                after = before
                padded[r, :, chan:2 * chan] = values.reshape(rows, chan).astype(jnp.bfloat16)
            else:
                span = slice((r - 1) * rows, r * rows)
                values = joined(hidden, span).reshape(rows // 8, 8, chan)
                before = joined(left, span).reshape(rows // 8, 8, chan)
                after = joined(right, span).reshape(rows // 8, 8, chan)
            lower = jnp.where(first, before, pltpu.roll(values, 1, 1))
            upper = jnp.where(last, after, pltpu.roll(values, 7, 1))
            padded[r, :, 0:chan] = lower.reshape(rows, chan).astype(jnp.bfloat16)
            padded[r, :, 2 * chan:3 * chan] = upper.reshape(rows, chan).astype(jnp.bfloat16)

        step = 2

        @pl.loop(0, side // step)
        def _(part):
            r = part * step
            total = jnp.broadcast_to(biases[layer:layer + 1, :], (step * rows, chan))
            for i in range(3):
                total += jnp.dot(
                    padded[pl.ds(r + i, step)].reshape(step * rows, 3 * chan),
                    weights[layer, i],
                    preferred_element_type=jnp.float32,
                )
            if layer == 0:
                total += jnp.dot(
                    skip_in[m, pl.ds(r, step)].reshape(step * rows, chan),
                    skip_w[...],
                    preferred_element_type=jnp.float32,
                )
            value = 0.5 * total * (1.0 + lax.erf(total * np.float32(0.5 ** 0.5)))
            if layer == LAYERS - 1:
                out[m, pl.ds(r, step)] = value.reshape(step, rows, chan).astype(jnp.bfloat16)
            else:
                split_store(hidden, pl.ds(pl.multiple_of(r * rows, 8), step * rows), value)

        for by in range(1, tiles):
            halo_copy(layer, by).wait_send()

    @pl.loop(0, micro)
    def _(m):
        @pl.when(section > 0)
        def _():
            chain_copy(m).wait_recv()

        @pl.when(section >= half)
        def _():
            skip_copy(m).wait_recv()

        for r in range(side):
            split_store(hidden, slice(r * rows, (r + 1) * rows), chain_in[m, r].astype(jnp.float32))
        for layer in range(LAYERS):
            run_layer(m, layer)

        @pl.when(section < sections - 1)
        def _():
            chain_copy(m).start()

        @pl.when(section < sections - half)
        def _():
            skip_copy(m).start()

    @pl.loop(0, micro)
    def _(m):
        @pl.when(section < sections - 1)
        def _():
            chain_copy(m).wait_send()

        @pl.when(section < sections - half)
        def _():
            skip_copy(m).wait_send()


def on_device(states, conv_weight, skip_weight, bias, placement):
    sections = lax.axis_size("section")
    tiles = lax.axis_size("tile")
    device = lax.axis_index("tile")
    micro, patches, side, _, chan = states.shape
    neighbour, rim_side, flip_flag = seam_tables(PR)
    assert not flip_flag.any()
    send_row, _, recv_dev, recv_slot = off_device_routes(neighbour, rim_side, flip_flag, tiles, patches)
    slots = send_row.shape[2]
    whole = patches + patches % 2
    rows = whole * side
    my_block = placement[device]
    order = jnp.arange(tiles, dtype=jnp.int32)
    owner = jnp.zeros((tiles,), jnp.int32).at[placement].set(order)
    to_block = placement[(device + order) % tiles]
    send_rows = jnp.asarray(send_row)[my_block][to_block].reshape(-1)
    source = jnp.asarray(recv_dev)[my_block].reshape(-1)
    recv_self = (source == my_block).astype(jnp.int32)
    by = (device - owner[source] + tiles) % tiles
    recv_from = jnp.maximum(by - 1, 0).astype(jnp.int32)
    recv_row = jnp.asarray(recv_slot)[my_block].reshape(-1)

    ordered = states.transpose(0, 2, 1, 3, 4)
    if whole != patches:
        ordered = jnp.pad(ordered, ((0, 0), (0, 0), (0, whole - patches), (0, 0), (0, 0)))
    ordered = ordered.reshape(micro, side, rows, chan)
    weights = conv_weight[0].reshape(LAYERS, 3, 3 * chan, chan)
    smem = pl.BlockSpec(memory_space=pltpu.SMEM)
    vmem = pl.BlockSpec(memory_space=pltpu.VMEM)
    field = pltpu.VMEM((micro, side, rows, chan), jnp.bfloat16)
    wide = pltpu.VMEM((chan // LANES, side * rows, LANES), jnp.float32)
    edge = pltpu.VMEM((rows, chan), jnp.float32)
    got = pltpu.VMEM((tiles - 1, slots, side, chan), jnp.bfloat16)
    flops = 2 * micro * side * rows * chan * chan * (9 * LAYERS + 1)
    result = pl.pallas_call(
        functools.partial(window_kernel, tiles, sections, patches, micro, slots),
        out_shape=jax.ShapeDtypeStruct((micro, side, rows, chan), jnp.bfloat16),
        in_specs=[smem] * 4 + [vmem] * 4,
        out_specs=vmem,
        scratch_shapes=[
            field, field, wide, wide, wide,
            pltpu.VMEM((side + 2, rows, 3 * chan), jnp.bfloat16),
            edge, edge,
            pltpu.VMEM((patches * 4, side, chan), jnp.float32),
            pltpu.VMEM((2, tiles - 1, slots, side, chan), jnp.bfloat16),
            got, got,
            pltpu.SemaphoreType.DMA((2, tiles - 1)),
            pltpu.SemaphoreType.DMA((2, tiles - 1)),
            pltpu.SemaphoreType.DMA((2, micro)),
            pltpu.SemaphoreType.DMA((2, micro)),
        ],
        compiler_params=pltpu.CompilerParams(
            collective_id=0, has_side_effects=True, vmem_limit_bytes=56 * 1024 * 1024
        ),
        cost_estimate=pl.CostEstimate(flops=flops, bytes_accessed=2**24, transcendentals=0),
    )(
        send_rows, recv_self, recv_from, recv_row,
        ordered, weights, skip_weight[0], bias[0].astype(jnp.float32),
    )
    result = result.reshape(micro, side, whole, side, chan)[:, :, :patches]
    return result.transpose(0, 2, 1, 3, 4)[None]


def solution(mesh):
    in_specs = (
        P(None, "tile", None, None, None),
        P("section", None, None, None, None, None),
        P("section", None, None),
        P("section", None, None),
        P(),
    )
    out_specs = P("section", None, "tile", None, None, None)
    return jax.shard_map(
        on_device, mesh=mesh, in_specs=in_specs, out_specs=out_specs, check_vma=False
    )
```

```python
import functools

import jax
import jax.numpy as jnp
import numpy as np
from jax import lax
from jax.experimental import pallas as pl
from jax.experimental.pallas import tpu as pltpu
from jax.sharding import PartitionSpec as P

LAYERS = 2
PR = 4


def face_across(face_num, direction):
    cycle = face_num // 4
    column = face_num % 4
    if cycle == 0:
        table = [4 + column, 4 + (column + 1) % 4, (column + 1) % 4, (column + 3) % 4]
    elif cycle == 1:
        table = [8 + (column + 3) % 4, 8 + column, column, (column + 3) % 4]
    else:
        table = [8 + (column + 3) % 4, 8 + (column + 1) % 4, 4 + (column + 1) % 4, 4 + column]
    return table[direction]


def locate(face_num, coord_x, coord_y, face_span):
    if 0 <= coord_x < face_span and 0 <= coord_y < face_span:
        return (face_num, coord_x, coord_y)
    if coord_x < 0:
        direction = 0
    elif coord_y < 0:
        direction = 1
    elif coord_x >= face_span:
        direction = 2
    else:
        direction = 3
    cycle = face_num // 4
    target = face_across(face_num, direction)
    coord_x = coord_x % face_span
    coord_y = coord_y % face_span
    if cycle == 0 and direction == 2 or (cycle == 2 and direction == 0):
        coord_x, coord_y = (coord_y, face_span - 1 - coord_x)
    elif cycle == 0 and direction == 3 or (cycle == 2 and direction == 1):
        coord_x, coord_y = (face_span - 1 - coord_y, coord_x)
    return (target, coord_x, coord_y)


def seam_tables(tiles):
    cell_side = 2
    face_span = tiles * cell_side
    face_tiles = tiles * tiles
    total = 12 * face_tiles
    neighbour = np.zeros((total, 4), np.int32)
    rim_side = np.zeros((total, 4), np.int32)
    flip_flag = np.zeros((total, 4), np.int32)
    for patch_num in range(total):
        cycle = patch_num % 3
        rest = patch_num // 3
        column = rest // face_tiles
        tile_y = rest % face_tiles // tiles
        tile_x = rest % tiles
        face_num = 4 * cycle + column
        base_x = tile_x * cell_side
        base_y = tile_y * cell_side
        for side_num in range(4):
            found = []
            for step_num in range(2):
                if side_num == 0:
                    point = (base_x - 1, base_y + step_num)
                elif side_num == 1:
                    point = (base_x + cell_side, base_y + step_num)
                elif side_num == 2:
                    point = (base_x + step_num, base_y - 1)
                else:
                    point = (base_x + step_num, base_y + cell_side)
                found.append(locate(face_num, point[0], point[1], face_span))
            face_a, first_x, first_y = found[0]
            face_b, second_x, second_y = found[1]
            neighbour[patch_num, side_num] = (
                3 * (face_a % 4 * face_tiles + first_y // cell_side * tiles + first_x // cell_side)
                + face_a // 4
            )
            if first_x == second_x:
                rim_side[patch_num, side_num] = 0 if first_x % cell_side == 0 else 1
                flip_flag[patch_num, side_num] = 1 if second_y < first_y else 0
            else:
                rim_side[patch_num, side_num] = 2 if first_y % cell_side == 0 else 3
                flip_flag[patch_num, side_num] = 1 if second_x < first_x else 0
    return (neighbour, rim_side, flip_flag)


def off_device_routes(neighbour, rim_side, flip_flag, tile_count, per_dev):
    source_dev = (neighbour // per_dev).reshape(-1)
    dest_dev = np.repeat(np.arange(neighbour.shape[0]) // per_dev, 4)
    row = (neighbour % per_dev * 4 + rim_side).reshape(-1)
    away = source_dev != dest_dev
    slot_num = np.zeros(row.shape[0], np.int64)
    counts = np.zeros((tile_count, tile_count), np.int64)
    for e in np.flatnonzero(away):
        slot_num[e] = counts[source_dev[e], dest_dev[e]]
        counts[source_dev[e], dest_dev[e]] += 1
    send_row = np.zeros((tile_count, tile_count, int(counts.max())), np.int32)
    send_row[source_dev[away], dest_dev[away], slot_num[away]] = row[away]
    place = np.where(away, slot_num, row)
    recv_dev = source_dev.reshape(tile_count, per_dev, 4).astype(np.int32)
    recv_slot = place.reshape(tile_count, per_dev, 4).astype(np.int32)
    return (send_row, None, recv_dev, recv_slot)


MESH = pl.DeviceIdType.MESH
LANES = 128


def joined(ref, span):
    return jnp.concatenate([ref[b, span, :] for b in range(ref.shape[0])], axis=1)


def split_store(ref, span, value):
    for b in range(ref.shape[0]):
        ref[b, span, :] = value[:, b * LANES:(b + 1) * LANES]


def window_kernel(
    tiles, sections, patches, micro, slots,
    placement, table,
    states, weights, skip_w, biases,
    out,
    chain_in, skip_in, hidden, summed, padded, edges, rims,
    outgoing, received_a, received_b, behind,
    halo_send, halo_recv, move_send, move_recv,
):
    tile = lax.axis_index("tile")
    section = lax.axis_index("section")
    half = sections // 2
    side = states.shape[1]
    rows = states.shape[2]
    chan = states.shape[3]
    received = (received_a, received_b)

    def tile_at(by):
        return lax.rem(tile + by, tiles)

    barrier = pltpu.get_barrier_semaphore()
    for by in range(1, tiles):
        pl.semaphore_signal(barrier, inc=1, device_id={"tile": tile_at(by)}, device_id_type=MESH)
    for by in range(1, sections):
        pl.semaphore_signal(
            barrier, inc=1, device_id={"section": lax.rem(section + by, sections)}, device_id_type=MESH
        )
    pl.semaphore_wait(barrier, tiles - 1 + sections - 1)

    my_block = placement[tile]
    sources = tiles * tiles * slots + my_block * (4 * patches)
    places = sources + tiles * 4 * patches

    @pl.loop(0, tiles)
    def _(block):
        def one(by, found):
            here = placement[lax.rem(tile - by + tiles, tiles)]
            return jnp.where(here == block, by, found)

        behind[block] = lax.fori_loop(0, tiles, one, jnp.int32(0))

    nothing = jnp.zeros((rows, 3 * chan), jnp.bfloat16)
    padded[0] = nothing
    padded[side + 1] = nothing

    @pl.when(section == 0)
    def _():
        chain_in[...] = states[...]

    @pl.when(section < half)
    def _():
        skip_in[...] = states[...]

    column = lax.broadcasted_iota(jnp.int32, (rows // 8, 8, chan), 1)
    first = column == 0
    last = column == 7

    def halo_copy(layer, by):
        return pltpu.make_async_remote_copy(
            src_ref=outgoing.at[layer, by - 1],
            dst_ref=received[layer].at[by - 1],
            send_sem=halo_send.at[layer, by - 1],
            recv_sem=halo_recv.at[layer, by - 1],
            device_id={"tile": tile_at(by)},
            device_id_type=MESH,
        )

    def chain_copy(m):
        return pltpu.make_async_remote_copy(
            src_ref=out.at[m], dst_ref=chain_in.at[m],
            send_sem=move_send.at[0, m], recv_sem=move_recv.at[0, m],
            device_id={"section": lax.rem(section + 1, sections)}, device_id_type=MESH,
        )

    def skip_copy(m):
        return pltpu.make_async_remote_copy(
            src_ref=out.at[m], dst_ref=skip_in.at[m],
            send_sem=move_send.at[1, m], recv_sem=move_recv.at[1, m],
            device_id={"section": lax.rem(section + half, sections)}, device_id_type=MESH,
        )

    def gelu(z):
        return 0.5 * z * (1.0 + lax.erf(z * np.float32(0.5 ** 0.5)))

    def shifted(values):
        cells = values.reshape(rows // 8, 8, chan)
        lower = jnp.where(first, 0.0, pltpu.roll(cells, 1, 1)).reshape(rows, chan)
        upper = jnp.where(last, 0.0, pltpu.roll(cells, 7, 1)).reshape(rows, chan)
        return jnp.concatenate([lower, values, upper], axis=1).astype(jnp.bfloat16)

    def run_layer(m, layer):
        for p in range(patches):
            top = (side - 1) * rows + p * 8
            for b in range(chan // LANES):
                lanes = slice(b * LANES, (b + 1) * LANES)
                rims[4 * p, :, lanes] = hidden[b, pl.ds(p * 8, 8, stride=rows), :]
                rims[4 * p + 1, :, lanes] = hidden[b, pl.ds(p * 8 + 7, 8, stride=rows), :]
                rims[4 * p + 2, :, lanes] = hidden[b, p * 8:p * 8 + 8, :]
                rims[4 * p + 3, :, lanes] = hidden[b, top:top + 8, :]
        for by in range(1, tiles):
            base = (my_block * tiles + placement[tile_at(by)]) * slots
            for q in range(slots):
                outgoing[layer, by - 1, q] = rims[table[base + q]].astype(jnp.bfloat16)
            halo_copy(layer, by).start()

        for r in range(side):
            values = joined(hidden, slice(r * rows, (r + 1) * rows))
            padded[r + 1] = shifted(values)

        step = 2

        @pl.loop(0, side // step)
        def _(part):
            r = part * step
            total = jnp.broadcast_to(biases[layer:layer + 1, :], (step * rows, chan))
            for i in range(3):
                total += jnp.dot(
                    padded[pl.ds(r + i, step)].reshape(step * rows, 3 * chan),
                    weights[layer, i],
                    preferred_element_type=jnp.float32,
                )
            if layer == 0:
                total += jnp.dot(
                    skip_in[m, pl.ds(r, step)].reshape(step * rows, chan),
                    skip_w[...],
                    preferred_element_type=jnp.float32,
                )
            span = pl.ds(pl.multiple_of(r * rows, 8), step * rows)
            split_store(summed, span, total)
            split_store(hidden, span, gelu(total))

        for by in range(1, tiles):
            halo_copy(layer, by).wait_recv()
        for e in range(4 * patches):
            by = behind[table[sources + e]]
            row = table[places + e]
            edges[e % 4, e // 4 * 8:e // 4 * 8 + 8, :] = jnp.where(
                by == 0,
                rims[row],
                received[layer][jnp.maximum(by - 1, 0), lax.rem(row, slots)].astype(jnp.float32),
            )
        for k in (2, 3):
            row = 0 if k == 2 else side - 1
            added = jnp.dot(
                shifted(edges[k]), weights[layer, k * 2 - 4], preferred_element_type=jnp.float32
            )
            span = slice(row * rows, (row + 1) * rows)
            total = joined(summed, span) + added
            split_store(summed, span, total)
            split_store(hidden, span, gelu(total))
        for k in (0, 1):
            moved = shifted(edges[k])
            added = jnp.zeros((rows, chan), jnp.float32)
            for i in range(3):
                added += jnp.dot(
                    moved[:, i * chan:(i + 1) * chan],
                    weights[layer, i, k * 2 * chan:(k * 2 + 1) * chan],
                    preferred_element_type=jnp.float32,
                )
            for p in range(patches):
                span = pl.ds(p * 8 + k * 7, 8, stride=rows)
                for b in range(chan // LANES):
                    part = added[p * 8:p * 8 + 8, b * LANES:(b + 1) * LANES]
                    hidden[b, span, :] = gelu(summed[b, span, :] + part)
        if layer == LAYERS - 1:
            for r in range(side):
                out[m, r] = joined(hidden, slice(r * rows, (r + 1) * rows)).astype(jnp.bfloat16)
        for by in range(1, tiles):
            halo_copy(layer, by).wait_send()

    @pl.loop(0, micro)
    def _(m):
        @pl.when(section > 0)
        def _():
            chain_copy(m).wait_recv()

        @pl.when(section >= half)
        def _():
            skip_copy(m).wait_recv()

        for r in range(side):
            split_store(hidden, slice(r * rows, (r + 1) * rows), chain_in[m, r].astype(jnp.float32))
        for layer in range(LAYERS):
            run_layer(m, layer)

        @pl.when(section < sections - 1)
        def _():
            chain_copy(m).start()

        @pl.when(section < sections - half)
        def _():
            skip_copy(m).start()

    @pl.loop(0, micro)
    def _(m):
        @pl.when(section < sections - 1)
        def _():
            chain_copy(m).wait_send()

        @pl.when(section < sections - half)
        def _():
            skip_copy(m).wait_send()


def on_device(states, conv_weight, skip_weight, bias, placement):
    sections = lax.axis_size("section")
    tiles = lax.axis_size("tile")
    micro, patches, side, _, chan = states.shape
    neighbour, rim_side, flip_flag = seam_tables(PR)
    assert not flip_flag.any()
    send_row, _, recv_dev, recv_slot = off_device_routes(neighbour, rim_side, flip_flag, tiles, patches)
    slots = send_row.shape[2]
    whole = patches + patches % 2
    rows = whole * side
    table = np.concatenate([x.reshape(-1) for x in (send_row, recv_dev, recv_slot)])
    ordered = states.transpose(0, 2, 1, 3, 4)
    if whole != patches:
        ordered = jnp.pad(ordered, ((0, 0), (0, 0), (0, whole - patches), (0, 0), (0, 0)))
    ordered = ordered.reshape(micro, side, rows, chan)
    weights = conv_weight[0].reshape(LAYERS, 3, 3 * chan, chan)
    smem = pl.BlockSpec(memory_space=pltpu.SMEM)
    vmem = pl.BlockSpec(memory_space=pltpu.VMEM)
    field = pltpu.VMEM((micro, side, rows, chan), jnp.bfloat16)
    wide = pltpu.VMEM((chan // LANES, side * rows, LANES), jnp.float32)
    got = pltpu.VMEM((tiles - 1, slots, side, chan), jnp.bfloat16)
    flops = 2 * micro * side * rows * chan * chan * (9 * LAYERS + 1)
    result = pl.pallas_call(
        functools.partial(window_kernel, tiles, sections, patches, micro, slots),
        out_shape=jax.ShapeDtypeStruct((micro, side, rows, chan), jnp.bfloat16),
        in_specs=[smem] * 2 + [vmem] * 4,
        out_specs=vmem,
        scratch_shapes=[
            field, field, wide, wide,
            pltpu.VMEM((side + 2, rows, 3 * chan), jnp.bfloat16),
            pltpu.VMEM((4, rows, chan), jnp.float32),
            pltpu.VMEM((patches * 4, side, chan), jnp.float32),
            pltpu.VMEM((2, tiles - 1, slots, side, chan), jnp.bfloat16),
            got, got,
            pltpu.SMEM((tiles,), jnp.int32),
            pltpu.SemaphoreType.DMA((2, tiles - 1)),
            pltpu.SemaphoreType.DMA((2, tiles - 1)),
            pltpu.SemaphoreType.DMA((2, micro)),
            pltpu.SemaphoreType.DMA((2, micro)),
        ],
        compiler_params=pltpu.CompilerParams(
            collective_id=0, has_side_effects=True, vmem_limit_bytes=56 * 1024 * 1024
        ),
        cost_estimate=pl.CostEstimate(flops=flops, bytes_accessed=2**24, transcendentals=0),
    )(
        placement, jnp.asarray(table, jnp.int32),
        ordered, weights, skip_weight[0], bias[0].astype(jnp.float32),
    )
    result = result.reshape(micro, side, whole, side, chan)[:, :, :patches]
    return result.transpose(0, 2, 1, 3, 4)[None]


def solution(mesh):
    in_specs = (
        P(None, "tile", None, None, None),
        P("section", None, None, None, None, None),
        P("section", None, None),
        P("section", None, None),
        P(),
    )
    out_specs = P("section", None, "tile", None, None, None)
    return jax.shard_map(
        on_device, mesh=mesh, in_specs=in_specs, out_specs=out_specs, check_vma=False
    )
```

```python
import functools

import jax
import jax.numpy as jnp
import numpy as np
from jax import lax
from jax.experimental import pallas as pl
from jax.experimental.pallas import tpu as pltpu
from jax.sharding import PartitionSpec as P

LAYERS = 2
PR = 4


def face_across(face_num, direction):
    cycle = face_num // 4
    column = face_num % 4
    if cycle == 0:
        table = [4 + column, 4 + (column + 1) % 4, (column + 1) % 4, (column + 3) % 4]
    elif cycle == 1:
        table = [8 + (column + 3) % 4, 8 + column, column, (column + 3) % 4]
    else:
        table = [8 + (column + 3) % 4, 8 + (column + 1) % 4, 4 + (column + 1) % 4, 4 + column]
    return table[direction]


def locate(face_num, coord_x, coord_y, face_span):
    if 0 <= coord_x < face_span and 0 <= coord_y < face_span:
        return (face_num, coord_x, coord_y)
    if coord_x < 0:
        direction = 0
    elif coord_y < 0:
        direction = 1
    elif coord_x >= face_span:
        direction = 2
    else:
        direction = 3
    cycle = face_num // 4
    target = face_across(face_num, direction)
    coord_x = coord_x % face_span
    coord_y = coord_y % face_span
    if cycle == 0 and direction == 2 or (cycle == 2 and direction == 0):
        coord_x, coord_y = (coord_y, face_span - 1 - coord_x)
    elif cycle == 0 and direction == 3 or (cycle == 2 and direction == 1):
        coord_x, coord_y = (face_span - 1 - coord_y, coord_x)
    return (target, coord_x, coord_y)


def seam_tables(tiles):
    cell_side = 2
    face_span = tiles * cell_side
    face_tiles = tiles * tiles
    total = 12 * face_tiles
    neighbour = np.zeros((total, 4), np.int32)
    rim_side = np.zeros((total, 4), np.int32)
    flip_flag = np.zeros((total, 4), np.int32)
    for patch_num in range(total):
        cycle = patch_num % 3
        rest = patch_num // 3
        column = rest // face_tiles
        tile_y = rest % face_tiles // tiles
        tile_x = rest % tiles
        face_num = 4 * cycle + column
        base_x = tile_x * cell_side
        base_y = tile_y * cell_side
        for side_num in range(4):
            found = []
            for step_num in range(2):
                if side_num == 0:
                    point = (base_x - 1, base_y + step_num)
                elif side_num == 1:
                    point = (base_x + cell_side, base_y + step_num)
                elif side_num == 2:
                    point = (base_x + step_num, base_y - 1)
                else:
                    point = (base_x + step_num, base_y + cell_side)
                found.append(locate(face_num, point[0], point[1], face_span))
            face_a, first_x, first_y = found[0]
            face_b, second_x, second_y = found[1]
            neighbour[patch_num, side_num] = (
                3 * (face_a % 4 * face_tiles + first_y // cell_side * tiles + first_x // cell_side)
                + face_a // 4
            )
            if first_x == second_x:
                rim_side[patch_num, side_num] = 0 if first_x % cell_side == 0 else 1
                flip_flag[patch_num, side_num] = 1 if second_y < first_y else 0
            else:
                rim_side[patch_num, side_num] = 2 if first_y % cell_side == 0 else 3
                flip_flag[patch_num, side_num] = 1 if second_x < first_x else 0
    return (neighbour, rim_side, flip_flag)


def off_device_routes(neighbour, rim_side, flip_flag, tile_count, per_dev):
    source_dev = (neighbour // per_dev).reshape(-1)
    dest_dev = np.repeat(np.arange(neighbour.shape[0]) // per_dev, 4)
    row = (neighbour % per_dev * 4 + rim_side).reshape(-1)
    away = source_dev != dest_dev
    slot_num = np.zeros(row.shape[0], np.int64)
    counts = np.zeros((tile_count, tile_count), np.int64)
    for e in np.flatnonzero(away):
        slot_num[e] = counts[source_dev[e], dest_dev[e]]
        counts[source_dev[e], dest_dev[e]] += 1
    send_row = np.zeros((tile_count, tile_count, int(counts.max())), np.int32)
    send_row[source_dev[away], dest_dev[away], slot_num[away]] = row[away]
    place = np.where(away, slot_num, row)
    recv_dev = source_dev.reshape(tile_count, per_dev, 4).astype(np.int32)
    recv_slot = place.reshape(tile_count, per_dev, 4).astype(np.int32)
    return (send_row, None, recv_dev, recv_slot)


MESH = pl.DeviceIdType.MESH
LANES = 128


def joined(ref, span):
    return jnp.concatenate([ref[b, span, :] for b in range(ref.shape[0])], axis=1)


def split_store(ref, span, value):
    for b in range(ref.shape[0]):
        ref[b, span, :] = value[:, b * LANES:(b + 1) * LANES]


def window_kernel(
    tiles, sections, patches, micro, slots,
    placement, table,
    states, weights, skip_w, biases,
    out,
    held, skip_held, bias_held, stage, hidden, summed, padded, edges, rims,
    outgoing, received_a, received_b, behind,
    halo_send, halo_recv, weight_send, weight_recv, own_sem, out_send, out_recv, ready,
):
    tile = lax.axis_index("tile")
    section = lax.axis_index("section")
    half = sections // 2
    side = states.shape[1]
    rows = states.shape[2]
    chan = states.shape[3]
    received = (received_a, received_b)

    def tile_at(by):
        return lax.rem(tile + by, tiles)

    barrier = pltpu.get_barrier_semaphore()
    for by in range(1, tiles):
        pl.semaphore_signal(barrier, inc=1, device_id={"tile": tile_at(by)}, device_id_type=MESH)
    for by in range(1, sections):
        pl.semaphore_signal(
            barrier, inc=1, device_id={"section": lax.rem(section + by, sections)}, device_id_type=MESH
        )
    pl.semaphore_wait(barrier, tiles - 1 + sections - 1)

    group = sections // micro
    works = lax.rem(section, group) == 0
    mine = section // group
    my_block = placement[tile]
    sources = tiles * tiles * slots + my_block * (4 * patches)
    places = sources + tiles * 4 * patches

    @pl.loop(0, tiles)
    def _(block):
        def one(by, found):
            here = placement[lax.rem(tile - by + tiles, tiles)]
            return jnp.where(here == block, by, found)

        behind[block] = lax.fori_loop(0, tiles, one, jnp.int32(0))

    nothing = jnp.zeros((rows, 3 * chan), jnp.bfloat16)
    padded[0] = nothing
    padded[side + 1] = nothing

    column = lax.broadcasted_iota(jnp.int32, (rows // 8, 8, chan), 1)
    first = column == 0
    last = column == 7

    def halo_copy(layer, by):
        return pltpu.make_async_remote_copy(
            src_ref=outgoing.at[layer, by - 1],
            dst_ref=received[layer].at[by - 1],
            send_sem=halo_send.at[layer, by - 1],
            recv_sem=halo_recv.at[layer, by - 1],
            device_id={"tile": tile_at(by)},
            device_id_type=MESH,
        )

    pieces = ((weights.at[0], held, 0), (weights.at[1], held, 1), (skip_w, skip_held, None), (biases, bias_held, None))

    def weight_copy(piece, source, worker):
        src, dst, layer = pieces[piece]
        return pltpu.make_async_remote_copy(
            src_ref=src,
            dst_ref=dst.at[source] if layer is None else dst.at[source, layer],
            send_sem=weight_send.at[worker, piece],
            recv_sem=weight_recv.at[source, piece],
            device_id={"section": worker * group},
            device_id_type=MESH,
        )

    def own_copy(piece):
        src, dst, layer = pieces[piece]
        return pltpu.make_async_copy(
            src, dst.at[section] if layer is None else dst.at[section, layer], own_sem.at[piece]
        )

    def out_copy(m, sec):
        return pltpu.make_async_remote_copy(
            src_ref=stage.at[half + sec], dst_ref=out.at[m],
            send_sem=out_send.at[sec], recv_sem=out_recv.at[m],
            device_id={"section": sec}, device_id_type=MESH,
        )

    def need(piece, sec):
        @pl.when(sec == section)
        def _():
            own_copy(piece).wait()

        @pl.when(sec != section)
        def _():
            weight_copy(piece, sec, 0).wait_recv()

    def gelu(z):
        return 0.5 * z * (1.0 + lax.erf(z * np.float32(0.5 ** 0.5)))

    def shifted(values):
        cells = values.reshape(rows // 8, 8, chan)
        lower = jnp.where(first, 0.0, pltpu.roll(cells, 1, 1)).reshape(rows, chan)
        upper = jnp.where(last, 0.0, pltpu.roll(cells, 7, 1)).reshape(rows, chan)
        return jnp.concatenate([lower, values, upper], axis=1).astype(jnp.bfloat16)

    def run_layer(sec, layer):
        for p in range(patches):
            top = (side - 1) * rows + p * 8
            for b in range(chan // LANES):
                lanes = slice(b * LANES, (b + 1) * LANES)
                rims[4 * p, :, lanes] = hidden[b, pl.ds(p * 8, 8, stride=rows), :]
                rims[4 * p + 1, :, lanes] = hidden[b, pl.ds(p * 8 + 7, 8, stride=rows), :]
                rims[4 * p + 2, :, lanes] = hidden[b, p * 8:p * 8 + 8, :]
                rims[4 * p + 3, :, lanes] = hidden[b, top:top + 8, :]
        for by in range(1, tiles):
            base = (my_block * tiles + placement[tile_at(by)]) * slots
            for q in range(slots):
                outgoing[layer, by - 1, q] = rims[table[base + q]].astype(jnp.bfloat16)
            halo_copy(layer, by).start()

        for r in range(side):
            values = joined(hidden, slice(r * rows, (r + 1) * rows))
            padded[r + 1] = shifted(values)

        step = 2
        if layer == 0:
            need(3, sec)
            need(2, sec)
        need(layer, sec)
        if layer == LAYERS - 1:
            after = sec + 1

            @pl.when((after < sections) & (lax.rem(after, group) > 0) & (after // group != mine))
            def _():
                pl.semaphore_signal(
                    ready.at[mine], inc=1, device_id={"section": lax.rem(after, sections)},
                    device_id_type=MESH,
                )

        @pl.loop(0, side // step)
        def _(part):
            r = part * step
            total = jnp.broadcast_to(bias_held[sec, layer:layer + 1, :], (step * rows, chan))
            for i in range(3):
                total += jnp.dot(
                    padded[pl.ds(r + i, step)].reshape(step * rows, 3 * chan),
                    held[sec, layer, i],
                    preferred_element_type=jnp.float32,
                )
            if layer == 0:
                total += jnp.dot(
                    stage[sec, pl.ds(r, step)].reshape(step * rows, chan),
                    skip_held[sec],
                    preferred_element_type=jnp.float32,
                )
            span = pl.ds(pl.multiple_of(r * rows, 8), step * rows)
            split_store(summed, span, total)
            split_store(hidden, span, gelu(total))

        for by in range(1, tiles):
            halo_copy(layer, by).wait_recv()
        for e in range(4 * patches):
            by = behind[table[sources + e]]
            row = table[places + e]
            edges[e % 4, e // 4 * 8:e // 4 * 8 + 8, :] = jnp.where(
                by == 0,
                rims[row],
                received[layer][jnp.maximum(by - 1, 0), lax.rem(row, slots)].astype(jnp.float32),
            )
        for k in (2, 3):
            row = 0 if k == 2 else side - 1
            added = jnp.dot(
                shifted(edges[k]), held[sec, layer, k * 2 - 4], preferred_element_type=jnp.float32
            )
            span = slice(row * rows, (row + 1) * rows)
            total = joined(summed, span) + added
            split_store(summed, span, total)
            split_store(hidden, span, gelu(total))
        for k in (0, 1):
            moved = shifted(edges[k])
            added = jnp.zeros((rows, chan), jnp.float32)
            for i in range(3):
                added += jnp.dot(
                    moved[:, i * chan:(i + 1) * chan],
                    held[sec, layer, i, k * 2 * chan:(k * 2 + 1) * chan],
                    preferred_element_type=jnp.float32,
                )
            for p in range(patches):
                span = pl.ds(p * 8 + k * 7, 8, stride=rows)
                for b in range(chan // LANES):
                    part = added[p * 8:p * 8 + 8, b * LANES:(b + 1) * LANES]
                    hidden[b, span, :] = gelu(summed[b, span, :] + part)
        if layer == LAYERS - 1:
            for r in range(side):
                stage[half + sec, r] = joined(hidden, slice(r * rows, (r + 1) * rows)).astype(jnp.bfloat16)
        for by in range(1, tiles):
            halo_copy(layer, by).wait_send()

    def send_weights(worker, which):
        for piece in which:
            weight_copy(piece, section, worker).start()

    @pl.when(works)
    def _():
        for piece in (3, 2, 0, 1):
            own_copy(piece).start()

    for worker in range(micro):
        @pl.when((section != worker * group) & (works | (mine == worker)))
        def _():
            send_weights(worker, (3, 2, 0))

        @pl.when((section != worker * group) & (mine == worker))
        def _():
            send_weights(worker, (1,))

    for worker in range(micro):
        @pl.when(jnp.logical_not(works) & (mine != worker))
        def _():
            pl.semaphore_wait(ready.at[worker], 1)
            send_weights(worker, (3, 2, 0, 1))

    @pl.when(works)
    def _():
        for i in range(half):
            stage[i] = states[mine]
        for r in range(side):
            split_store(hidden, slice(r * rows, (r + 1) * rows), states[mine, r].astype(jnp.float32))

        @pl.loop(0, sections)
        def _(sec):
            for layer in range(LAYERS):
                run_layer(sec, layer)
                if layer == 0:
                    for worker in range(micro):
                        @pl.when((sec == 0) & (worker != mine))
                        def _():
                            send_weights(worker, (1,))

            @pl.when(sec == section)
            def _():
                out[mine] = stage[half + sec]

            @pl.when(sec != section)
            def _():
                out_copy(mine, sec).start()

        @pl.loop(0, sections)
        def _(sec):
            @pl.when(sec != section)
            def _():
                out_copy(mine, sec).wait_send()

    for worker in range(micro):
        @pl.when(section != worker * group)
        def _():
            for piece in range(4):
                weight_copy(piece, section, worker).wait_send()
            out_copy(worker, section).wait_recv()


def on_device(states, conv_weight, skip_weight, bias, placement):
    sections = lax.axis_size("section")
    tiles = lax.axis_size("tile")
    micro, patches, side, _, chan = states.shape
    neighbour, rim_side, flip_flag = seam_tables(PR)
    assert not flip_flag.any()
    send_row, _, recv_dev, recv_slot = off_device_routes(neighbour, rim_side, flip_flag, tiles, patches)
    slots = send_row.shape[2]
    whole = patches + patches % 2
    rows = whole * side
    table = np.concatenate([x.reshape(-1) for x in (send_row, recv_dev, recv_slot)])
    ordered = states.transpose(0, 2, 1, 3, 4)
    if whole != patches:
        ordered = jnp.pad(ordered, ((0, 0), (0, 0), (0, whole - patches), (0, 0), (0, 0)))
    ordered = ordered.reshape(micro, side, rows, chan)
    weights = conv_weight[0].reshape(LAYERS, 3, 3 * chan, chan)
    biases = jnp.pad(bias[0].astype(jnp.float32), ((0, 8 - LAYERS), (0, 0)))
    held = sections + sections // 2
    smem = pl.BlockSpec(memory_space=pltpu.SMEM)
    vmem = pl.BlockSpec(memory_space=pltpu.VMEM)
    wide = pltpu.VMEM((chan // LANES, side * rows, LANES), jnp.float32)
    got = pltpu.VMEM((tiles - 1, slots, side, chan), jnp.bfloat16)
    flops = 2 * micro * side * rows * chan * chan * (9 * LAYERS + 1)
    result = pl.pallas_call(
        functools.partial(window_kernel, tiles, sections, patches, micro, slots),
        out_shape=jax.ShapeDtypeStruct((micro, side, rows, chan), jnp.bfloat16),
        in_specs=[smem] * 2 + [vmem, pl.BlockSpec(memory_space=pl.ANY), vmem, vmem],
        out_specs=vmem,
        scratch_shapes=[
            pltpu.VMEM((sections,) + weights.shape, jnp.bfloat16),
            pltpu.VMEM((sections, chan, chan), jnp.bfloat16),
            pltpu.VMEM((sections, 8, chan), jnp.float32),
            pltpu.VMEM((held, side, rows, chan), jnp.bfloat16),
            wide, wide,
            pltpu.VMEM((side + 2, rows, 3 * chan), jnp.bfloat16),
            pltpu.VMEM((4, rows, chan), jnp.float32),
            pltpu.VMEM((patches * 4, side, chan), jnp.float32),
            pltpu.VMEM((2, tiles - 1, slots, side, chan), jnp.bfloat16),
            got, got,
            pltpu.SMEM((tiles,), jnp.int32),
            pltpu.SemaphoreType.DMA((2, tiles - 1)),
            pltpu.SemaphoreType.DMA((2, tiles - 1)),
            pltpu.SemaphoreType.DMA((micro, 4)),
            pltpu.SemaphoreType.DMA((sections, 4)),
            pltpu.SemaphoreType.DMA((4,)),
            pltpu.SemaphoreType.DMA((sections,)),
            pltpu.SemaphoreType.DMA((micro,)),
            pltpu.SemaphoreType.REGULAR((micro,)),
        ],
        compiler_params=pltpu.CompilerParams(
            collective_id=0, has_side_effects=True, vmem_limit_bytes=56 * 1024 * 1024
        ),
        cost_estimate=pl.CostEstimate(flops=flops, bytes_accessed=2**24, transcendentals=0),
    )(
        placement, jnp.asarray(table, jnp.int32),
        ordered, weights, skip_weight[0], biases,
    )
    result = result.reshape(micro, side, whole, side, chan)[:, :, :patches]
    return result.transpose(0, 2, 1, 3, 4)[None]


def solution(mesh):
    in_specs = (
        P(None, "tile", None, None, None),
        P("section", None, None, None, None, None),
        P("section", None, None),
        P("section", None, None),
        P(),
    )
    out_specs = P("section", None, "tile", None, None, None)
    return jax.shard_map(
        on_device, mesh=mesh, in_specs=in_specs, out_specs=out_specs, check_vma=False
    )
```

```python
import functools

import jax
import jax.numpy as jnp
import numpy as np
from jax import lax
from jax.experimental import pallas as pl
from jax.experimental.pallas import tpu as pltpu
from jax.sharding import PartitionSpec as P

LAYERS = 2
PR = 4


def face_across(face_num, direction):
    cycle = face_num // 4
    column = face_num % 4
    if cycle == 0:
        table = [4 + column, 4 + (column + 1) % 4, (column + 1) % 4, (column + 3) % 4]
    elif cycle == 1:
        table = [8 + (column + 3) % 4, 8 + column, column, (column + 3) % 4]
    else:
        table = [8 + (column + 3) % 4, 8 + (column + 1) % 4, 4 + (column + 1) % 4, 4 + column]
    return table[direction]


def locate(face_num, coord_x, coord_y, face_span):
    if 0 <= coord_x < face_span and 0 <= coord_y < face_span:
        return (face_num, coord_x, coord_y)
    if coord_x < 0:
        direction = 0
    elif coord_y < 0:
        direction = 1
    elif coord_x >= face_span:
        direction = 2
    else:
        direction = 3
    cycle = face_num // 4
    target = face_across(face_num, direction)
    coord_x = coord_x % face_span
    coord_y = coord_y % face_span
    if cycle == 0 and direction == 2 or (cycle == 2 and direction == 0):
        coord_x, coord_y = (coord_y, face_span - 1 - coord_x)
    elif cycle == 0 and direction == 3 or (cycle == 2 and direction == 1):
        coord_x, coord_y = (face_span - 1 - coord_y, coord_x)
    return (target, coord_x, coord_y)


def seam_tables(tiles):
    cell_side = 2
    face_span = tiles * cell_side
    face_tiles = tiles * tiles
    total = 12 * face_tiles
    neighbour = np.zeros((total, 4), np.int32)
    rim_side = np.zeros((total, 4), np.int32)
    flip_flag = np.zeros((total, 4), np.int32)
    for patch_num in range(total):
        cycle = patch_num % 3
        rest = patch_num // 3
        column = rest // face_tiles
        tile_y = rest % face_tiles // tiles
        tile_x = rest % tiles
        face_num = 4 * cycle + column
        base_x = tile_x * cell_side
        base_y = tile_y * cell_side
        for side_num in range(4):
            found = []
            for step_num in range(2):
                if side_num == 0:
                    point = (base_x - 1, base_y + step_num)
                elif side_num == 1:
                    point = (base_x + cell_side, base_y + step_num)
                elif side_num == 2:
                    point = (base_x + step_num, base_y - 1)
                else:
                    point = (base_x + step_num, base_y + cell_side)
                found.append(locate(face_num, point[0], point[1], face_span))
            face_a, first_x, first_y = found[0]
            face_b, second_x, second_y = found[1]
            neighbour[patch_num, side_num] = (
                3 * (face_a % 4 * face_tiles + first_y // cell_side * tiles + first_x // cell_side)
                + face_a // 4
            )
            if first_x == second_x:
                rim_side[patch_num, side_num] = 0 if first_x % cell_side == 0 else 1
                flip_flag[patch_num, side_num] = 1 if second_y < first_y else 0
            else:
                rim_side[patch_num, side_num] = 2 if first_y % cell_side == 0 else 3
                flip_flag[patch_num, side_num] = 1 if second_x < first_x else 0
    return (neighbour, rim_side, flip_flag)


def off_device_routes(neighbour, rim_side, flip_flag, tile_count, per_dev):
    source_dev = (neighbour // per_dev).reshape(-1)
    dest_dev = np.repeat(np.arange(neighbour.shape[0]) // per_dev, 4)
    row = (neighbour % per_dev * 4 + rim_side).reshape(-1)
    away = source_dev != dest_dev
    slot_num = np.zeros(row.shape[0], np.int64)
    counts = np.zeros((tile_count, tile_count), np.int64)
    for e in np.flatnonzero(away):
        slot_num[e] = counts[source_dev[e], dest_dev[e]]
        counts[source_dev[e], dest_dev[e]] += 1
    send_row = np.zeros((tile_count, tile_count, int(counts.max())), np.int32)
    send_row[source_dev[away], dest_dev[away], slot_num[away]] = row[away]
    place = np.where(away, slot_num, row)
    recv_dev = source_dev.reshape(tile_count, per_dev, 4).astype(np.int32)
    recv_slot = place.reshape(tile_count, per_dev, 4).astype(np.int32)
    return (send_row, None, recv_dev, recv_slot)


MESH = pl.DeviceIdType.MESH
LANES = 128


def joined(ref, span):
    return jnp.concatenate([ref[b, span, :] for b in range(ref.shape[0])], axis=1)


def split_store(ref, span, value):
    for b in range(ref.shape[0]):
        ref[b, span, :] = value[:, b * LANES:(b + 1) * LANES]


def window_kernel(
    tiles, sections, patches, micro, slots,
    placement, table,
    states, weights, skip_w, biases,
    out,
    held, skip_held, bias_held, stage, hidden, summed, padded, edges, rims,
    outgoing, received_a, received_b, behind,
    halo_send, halo_recv, weight_send, weight_recv, own_sem, out_send, out_recv, ready,
    relay_send, relay_recv, pass_send, pass_recv,
):
    tile = lax.axis_index("tile")
    section = lax.axis_index("section")
    half = sections // 2
    side = states.shape[1]
    rows = states.shape[2]
    chan = states.shape[3]
    received = (received_a, received_b)

    def tile_at(by):
        return lax.rem(tile + by, tiles)

    partner = tile + 1 - 2 * lax.rem(tile, 2)
    barrier = pltpu.get_barrier_semaphore()
    for by in range(1, tiles):
        pl.semaphore_signal(barrier, inc=1, device_id={"tile": tile_at(by)}, device_id_type=MESH)
    for by in range(1, sections):
        pl.semaphore_signal(
            barrier, inc=1, device_id={"section": lax.rem(section + by, sections)}, device_id_type=MESH
        )
        pl.semaphore_signal(
            barrier, inc=1, device_id={"tile": partner, "section": lax.rem(section + by, sections)},
            device_id_type=MESH,
        )
    pl.semaphore_wait(barrier, tiles - 1 + 2 * (sections - 1))

    group = sections // micro
    works = lax.rem(section, group) == 0
    mine = section // group
    my_block = placement[tile]
    sources = tiles * tiles * slots + my_block * (4 * patches)
    places = sources + tiles * 4 * patches

    @pl.loop(0, tiles)
    def _(block):
        def one(by, found):
            here = placement[lax.rem(tile - by + tiles, tiles)]
            return jnp.where(here == block, by, found)

        behind[block] = lax.fori_loop(0, tiles, one, jnp.int32(0))

    nothing = jnp.zeros((rows, 3 * chan), jnp.bfloat16)
    padded[0] = nothing
    padded[side + 1] = nothing

    column = lax.broadcasted_iota(jnp.int32, (rows // 8, 8, chan), 1)
    first = column == 0
    last = column == 7

    def halo_copy(layer, by):
        return pltpu.make_async_remote_copy(
            src_ref=outgoing.at[layer, by - 1],
            dst_ref=received[layer].at[by - 1],
            send_sem=halo_send.at[layer, by - 1],
            recv_sem=halo_recv.at[layer, by - 1],
            device_id={"tile": tile_at(by)},
            device_id_type=MESH,
        )

    pieces = ((weights.at[0], held, 0), (weights.at[1], held, 1), (skip_w, skip_held, None), (biases, bias_held, None))

    def weight_copy(piece, source, worker):
        src, dst, layer = pieces[piece]
        return pltpu.make_async_remote_copy(
            src_ref=src,
            dst_ref=dst.at[source] if layer is None else dst.at[source, layer],
            send_sem=weight_send.at[worker, piece],
            recv_sem=weight_recv.at[source, piece],
            device_id={"section": worker * group},
            device_id_type=MESH,
        )

    def own_copy(piece):
        src, dst, layer = pieces[piece]
        return pltpu.make_async_copy(
            src, dst.at[section] if layer is None else dst.at[section, layer], own_sem.at[piece]
        )

    def out_copy(m, sec):
        return pltpu.make_async_remote_copy(
            src_ref=stage.at[half + sec], dst_ref=out.at[m],
            send_sem=out_send.at[sec], recv_sem=out_recv.at[m],
            device_id={"section": sec}, device_id_type=MESH,
        )

    def need(piece, sec):
        @pl.when(sec == section)
        def _():
            own_copy(piece).wait()

        near = sec // group == mine

        @pl.when((sec != section) & (near if piece < 2 else True))
        def _():
            weight_copy(piece, sec, 0).wait_recv()

        if piece < 2:
            @pl.when(jnp.logical_not(near))
            def _():
                for hop in range(2):
                    pass_copy(piece, sec, hop, hop).wait_recv()

    deep = 3 * chan // 2

    def part(other):
        which = lax.rem(tile + other, 2)
        return pl.ds(pl.multiple_of(which * deep, LANES), deep)

    def relay_copy(layer, source, worker):
        return pltpu.make_async_remote_copy(
            src_ref=weights.at[layer, :, part(0)], dst_ref=held.at[source, layer, :, part(0)],
            send_sem=relay_send.at[worker, layer], recv_sem=relay_recv.at[source, layer],
            device_id={"section": worker * group + 1}, device_id_type=MESH,
        )

    def pass_copy(layer, source, hop, other):
        place = held.at[source, layer, :, part(other)]
        device = {"section": mine * group}
        if hop == 1:
            device["tile"] = partner
        return pltpu.make_async_remote_copy(
            src_ref=place, dst_ref=place,
            send_sem=pass_send.at[source, layer, hop], recv_sem=pass_recv.at[source, layer, hop],
            device_id=device, device_id_type=MESH,
        )

    def gelu(z):
        return 0.5 * z * (1.0 + lax.erf(z * np.float32(0.5 ** 0.5)))

    def shifted(values):
        cells = values.reshape(rows // 8, 8, chan)
        lower = jnp.where(first, 0.0, pltpu.roll(cells, 1, 1)).reshape(rows, chan)
        upper = jnp.where(last, 0.0, pltpu.roll(cells, 7, 1)).reshape(rows, chan)
        return jnp.concatenate([lower, values, upper], axis=1).astype(jnp.bfloat16)

    def run_layer(sec, layer):
        for p in range(patches):
            top = (side - 1) * rows + p * 8
            for b in range(chan // LANES):
                lanes = slice(b * LANES, (b + 1) * LANES)
                rims[4 * p, :, lanes] = hidden[b, pl.ds(p * 8, 8, stride=rows), :]
                rims[4 * p + 1, :, lanes] = hidden[b, pl.ds(p * 8 + 7, 8, stride=rows), :]
                rims[4 * p + 2, :, lanes] = hidden[b, p * 8:p * 8 + 8, :]
                rims[4 * p + 3, :, lanes] = hidden[b, top:top + 8, :]
        for by in range(1, tiles):
            base = (my_block * tiles + placement[tile_at(by)]) * slots
            for q in range(slots):
                outgoing[layer, by - 1, q] = rims[table[base + q]].astype(jnp.bfloat16)
            halo_copy(layer, by).start()

        for r in range(side):
            values = joined(hidden, slice(r * rows, (r + 1) * rows))
            padded[r + 1] = shifted(values)

        step = 2
        if layer == 0:
            need(3, sec)
            need(2, sec)
        need(layer, sec)
        @pl.loop(0, side // step)
        def _(part):
            r = part * step
            total = jnp.broadcast_to(bias_held[sec, layer:layer + 1, :], (step * rows, chan))
            for i in range(3):
                total += jnp.dot(
                    padded[pl.ds(r + i, step)].reshape(step * rows, 3 * chan),
                    held[sec, layer, i],
                    preferred_element_type=jnp.float32,
                )
            if layer == 0:
                total += jnp.dot(
                    stage[sec, pl.ds(r, step)].reshape(step * rows, chan),
                    skip_held[sec],
                    preferred_element_type=jnp.float32,
                )
            span = pl.ds(pl.multiple_of(r * rows, 8), step * rows)
            split_store(summed, span, total)
            split_store(hidden, span, gelu(total))

        for by in range(1, tiles):
            halo_copy(layer, by).wait_recv()
        for e in range(4 * patches):
            by = behind[table[sources + e]]
            row = table[places + e]
            edges[e % 4, e // 4 * 8:e // 4 * 8 + 8, :] = jnp.where(
                by == 0,
                rims[row],
                received[layer][jnp.maximum(by - 1, 0), lax.rem(row, slots)].astype(jnp.float32),
            )
        for k in (2, 3):
            row = 0 if k == 2 else side - 1
            added = jnp.dot(
                shifted(edges[k]), held[sec, layer, k * 2 - 4], preferred_element_type=jnp.float32
            )
            span = slice(row * rows, (row + 1) * rows)
            total = joined(summed, span) + added
            split_store(summed, span, total)
            split_store(hidden, span, gelu(total))
        for k in (0, 1):
            moved = shifted(edges[k])
            added = jnp.zeros((rows, chan), jnp.float32)
            for i in range(3):
                added += jnp.dot(
                    moved[:, i * chan:(i + 1) * chan],
                    held[sec, layer, i, k * 2 * chan:(k * 2 + 1) * chan],
                    preferred_element_type=jnp.float32,
                )
            for p in range(patches):
                span = pl.ds(p * 8 + k * 7, 8, stride=rows)
                for b in range(chan // LANES):
                    part = added[p * 8:p * 8 + 8, b * LANES:(b + 1) * LANES]
                    hidden[b, span, :] = gelu(summed[b, span, :] + part)
        if layer == LAYERS - 1:
            for r in range(side):
                stage[half + sec, r] = joined(hidden, slice(r * rows, (r + 1) * rows)).astype(jnp.bfloat16)
        for by in range(1, tiles):
            halo_copy(layer, by).wait_send()

    def send_weights(worker, which):
        for piece in which:
            weight_copy(piece, section, worker).start()

    @pl.when(works)
    def _():
        for piece in (3, 2, 0, 1):
            own_copy(piece).start()

    for worker in range(micro):
        @pl.when(section != worker * group)
        def _():
            send_weights(worker, (3, 2))

        @pl.when((section != worker * group) & (mine == worker))
        def _():
            send_weights(worker, (0, 1))

        @pl.when(works & (mine != worker))
        def _():
            for layer in range(LAYERS):
                relay_copy(layer, section, worker).start()

    relays = lax.rem(section, group) == 1

    def pass_on(source):
        for layer in range(LAYERS):
            relay_copy(layer, source, 0).wait_recv()
            for hop in range(2):
                pass_copy(layer, source, hop, 0).start()

    for rank in range(group):
        for worker in range(micro):
            source = worker * group + rank

            @pl.when(relays & (mine != worker))
            def _():
                pass_on(source)

        if rank + 1 < group:
            for worker in range(micro):
                @pl.when(relays & (mine != worker))
                def _():
                    pl.semaphore_signal(
                        ready.at[mine], inc=1, device_id={"section": worker * group + rank + 1},
                        device_id_type=MESH,
                    )

            for worker in range(micro):
                @pl.when((lax.rem(section, group) == rank + 1) & (mine != worker))
                def _():
                    pl.semaphore_wait(ready.at[worker], 1)
                    for layer in range(LAYERS):
                        relay_copy(layer, section, worker).start()

    @pl.when(works)
    def _():
        for i in range(half):
            stage[i] = states[mine]
        for r in range(side):
            split_store(hidden, slice(r * rows, (r + 1) * rows), states[mine, r].astype(jnp.float32))

        @pl.loop(0, sections)
        def _(sec):
            for layer in range(LAYERS):
                run_layer(sec, layer)

            @pl.when(sec == section)
            def _():
                out[mine] = stage[half + sec]

            @pl.when(sec != section)
            def _():
                out_copy(mine, sec).start()

        @pl.loop(0, sections)
        def _(sec):
            @pl.when(sec != section)
            def _():
                out_copy(mine, sec).wait_send()

    for worker in range(micro):
        @pl.when(section != worker * group)
        def _():
            for piece in (2, 3):
                weight_copy(piece, section, worker).wait_send()
            out_copy(worker, section).wait_recv()

        @pl.when((section != worker * group) & (mine == worker))
        def _():
            for piece in (0, 1):
                weight_copy(piece, section, worker).wait_send()

        @pl.when(mine != worker)
        def _():
            for layer in range(LAYERS):
                relay_copy(layer, section, worker).wait_send()

        @pl.when(relays & (mine != worker))
        def _():
            for rank in range(group):
                for layer in range(LAYERS):
                    for hop in range(2):
                        pass_copy(layer, worker * group + rank, hop, 0).wait_send()


def on_device(states, conv_weight, skip_weight, bias, placement):
    sections = lax.axis_size("section")
    tiles = lax.axis_size("tile")
    micro, patches, side, _, chan = states.shape
    neighbour, rim_side, flip_flag = seam_tables(PR)
    assert not flip_flag.any()
    send_row, _, recv_dev, recv_slot = off_device_routes(neighbour, rim_side, flip_flag, tiles, patches)
    slots = send_row.shape[2]
    whole = patches + patches % 2
    rows = whole * side
    table = np.concatenate([x.reshape(-1) for x in (send_row, recv_dev, recv_slot)])
    ordered = states.transpose(0, 2, 1, 3, 4)
    if whole != patches:
        ordered = jnp.pad(ordered, ((0, 0), (0, 0), (0, whole - patches), (0, 0), (0, 0)))
    ordered = ordered.reshape(micro, side, rows, chan)
    weights = conv_weight[0].reshape(LAYERS, 3, 3 * chan, chan)
    biases = jnp.pad(bias[0].astype(jnp.float32), ((0, 8 - LAYERS), (0, 0)))
    held = sections + sections // 2
    smem = pl.BlockSpec(memory_space=pltpu.SMEM)
    vmem = pl.BlockSpec(memory_space=pltpu.VMEM)
    wide = pltpu.VMEM((chan // LANES, side * rows, LANES), jnp.float32)
    got = pltpu.VMEM((tiles - 1, slots, side, chan), jnp.bfloat16)
    flops = 2 * micro * side * rows * chan * chan * (9 * LAYERS + 1)
    result = pl.pallas_call(
        functools.partial(window_kernel, tiles, sections, patches, micro, slots),
        out_shape=jax.ShapeDtypeStruct((micro, side, rows, chan), jnp.bfloat16),
        in_specs=[smem] * 2 + [vmem, pl.BlockSpec(memory_space=pl.ANY), vmem, vmem],
        out_specs=vmem,
        scratch_shapes=[
            pltpu.VMEM((sections,) + weights.shape, jnp.bfloat16),
            pltpu.VMEM((sections, chan, chan), jnp.bfloat16),
            pltpu.VMEM((sections, 8, chan), jnp.float32),
            pltpu.VMEM((held, side, rows, chan), jnp.bfloat16),
            wide, wide,
            pltpu.VMEM((side + 2, rows, 3 * chan), jnp.bfloat16),
            pltpu.VMEM((4, rows, chan), jnp.float32),
            pltpu.VMEM((patches * 4, side, chan), jnp.float32),
            pltpu.VMEM((2, tiles - 1, slots, side, chan), jnp.bfloat16),
            got, got,
            pltpu.SMEM((tiles,), jnp.int32),
            pltpu.SemaphoreType.DMA((2, tiles - 1)),
            pltpu.SemaphoreType.DMA((2, tiles - 1)),
            pltpu.SemaphoreType.DMA((micro, 4)),
            pltpu.SemaphoreType.DMA((sections, 4)),
            pltpu.SemaphoreType.DMA((4,)),
            pltpu.SemaphoreType.DMA((sections,)),
            pltpu.SemaphoreType.DMA((micro,)),
            pltpu.SemaphoreType.REGULAR((micro,)),
            pltpu.SemaphoreType.DMA((micro, LAYERS)),
            pltpu.SemaphoreType.DMA((sections, LAYERS)),
            pltpu.SemaphoreType.DMA((sections, LAYERS, 2)),
            pltpu.SemaphoreType.DMA((sections, LAYERS, 2)),
        ],
        compiler_params=pltpu.CompilerParams(
            collective_id=0, has_side_effects=True, vmem_limit_bytes=56 * 1024 * 1024
        ),
        cost_estimate=pl.CostEstimate(flops=flops, bytes_accessed=2**24, transcendentals=0),
    )(
        placement, jnp.asarray(table, jnp.int32),
        ordered, weights, skip_weight[0], biases,
    )
    result = result.reshape(micro, side, whole, side, chan)[:, :, :patches]
    return result.transpose(0, 2, 1, 3, 4)[None]


def solution(mesh):
    in_specs = (
        P(None, "tile", None, None, None),
        P("section", None, None, None, None, None),
        P("section", None, None),
        P("section", None, None),
        P(),
    )
    out_specs = P("section", None, "tile", None, None, None)
    return jax.shard_map(
        on_device, mesh=mesh, in_specs=in_specs, out_specs=out_specs, check_vma=False
    )
```

```python
import functools

import jax
import jax.numpy as jnp
import numpy as np
from jax import lax
from jax.experimental import pallas as pl
from jax.experimental.pallas import tpu as pltpu
from jax.sharding import PartitionSpec as P

LAYERS = 2
PR = 4


def face_across(face_num, direction):
    cycle = face_num // 4
    column = face_num % 4
    if cycle == 0:
        table = [4 + column, 4 + (column + 1) % 4, (column + 1) % 4, (column + 3) % 4]
    elif cycle == 1:
        table = [8 + (column + 3) % 4, 8 + column, column, (column + 3) % 4]
    else:
        table = [8 + (column + 3) % 4, 8 + (column + 1) % 4, 4 + (column + 1) % 4, 4 + column]
    return table[direction]


def locate(face_num, coord_x, coord_y, face_span):
    if 0 <= coord_x < face_span and 0 <= coord_y < face_span:
        return (face_num, coord_x, coord_y)
    if coord_x < 0:
        direction = 0
    elif coord_y < 0:
        direction = 1
    elif coord_x >= face_span:
        direction = 2
    else:
        direction = 3
    cycle = face_num // 4
    target = face_across(face_num, direction)
    coord_x = coord_x % face_span
    coord_y = coord_y % face_span
    if cycle == 0 and direction == 2 or (cycle == 2 and direction == 0):
        coord_x, coord_y = (coord_y, face_span - 1 - coord_x)
    elif cycle == 0 and direction == 3 or (cycle == 2 and direction == 1):
        coord_x, coord_y = (face_span - 1 - coord_y, coord_x)
    return (target, coord_x, coord_y)


def seam_tables(tiles):
    cell_side = 2
    face_span = tiles * cell_side
    face_tiles = tiles * tiles
    total = 12 * face_tiles
    neighbour = np.zeros((total, 4), np.int32)
    rim_side = np.zeros((total, 4), np.int32)
    flip_flag = np.zeros((total, 4), np.int32)
    for patch_num in range(total):
        cycle = patch_num % 3
        rest = patch_num // 3
        column = rest // face_tiles
        tile_y = rest % face_tiles // tiles
        tile_x = rest % tiles
        face_num = 4 * cycle + column
        base_x = tile_x * cell_side
        base_y = tile_y * cell_side
        for side_num in range(4):
            found = []
            for step_num in range(2):
                if side_num == 0:
                    point = (base_x - 1, base_y + step_num)
                elif side_num == 1:
                    point = (base_x + cell_side, base_y + step_num)
                elif side_num == 2:
                    point = (base_x + step_num, base_y - 1)
                else:
                    point = (base_x + step_num, base_y + cell_side)
                found.append(locate(face_num, point[0], point[1], face_span))
            face_a, first_x, first_y = found[0]
            face_b, second_x, second_y = found[1]
            neighbour[patch_num, side_num] = (
                3 * (face_a % 4 * face_tiles + first_y // cell_side * tiles + first_x // cell_side)
                + face_a // 4
            )
            if first_x == second_x:
                rim_side[patch_num, side_num] = 0 if first_x % cell_side == 0 else 1
                flip_flag[patch_num, side_num] = 1 if second_y < first_y else 0
            else:
                rim_side[patch_num, side_num] = 2 if first_y % cell_side == 0 else 3
                flip_flag[patch_num, side_num] = 1 if second_x < first_x else 0
    return (neighbour, rim_side, flip_flag)


def off_device_routes(neighbour, rim_side, flip_flag, tile_count, per_dev):
    source_dev = (neighbour // per_dev).reshape(-1)
    dest_dev = np.repeat(np.arange(neighbour.shape[0]) // per_dev, 4)
    row = (neighbour % per_dev * 4 + rim_side).reshape(-1)
    away = source_dev != dest_dev
    slot_num = np.zeros(row.shape[0], np.int64)
    counts = np.zeros((tile_count, tile_count), np.int64)
    for e in np.flatnonzero(away):
        slot_num[e] = counts[source_dev[e], dest_dev[e]]
        counts[source_dev[e], dest_dev[e]] += 1
    send_row = np.zeros((tile_count, tile_count, int(counts.max())), np.int32)
    send_row[source_dev[away], dest_dev[away], slot_num[away]] = row[away]
    place = np.where(away, slot_num, row)
    recv_dev = source_dev.reshape(tile_count, per_dev, 4).astype(np.int32)
    recv_slot = place.reshape(tile_count, per_dev, 4).astype(np.int32)
    return (send_row, None, recv_dev, recv_slot)


MESH = pl.DeviceIdType.MESH
LANES = 128


def joined(ref, span):
    return jnp.concatenate([ref[b, span, :] for b in range(ref.shape[0])], axis=1)


def split_store(ref, span, value):
    for b in range(ref.shape[0]):
        ref[b, span, :] = value[:, b * LANES:(b + 1) * LANES]


def window_kernel(
    tiles, sections, patches, micro, slots,
    placement, table,
    states, weights, skip_w, biases,
    out,
    held, skip_held, bias_held, stage, hidden, summed, padded, edges, rims,
    outgoing, received_a, received_b, behind,
    halo_send, halo_recv, weight_send, weight_recv, own_sem, out_send, out_recv, ready,
    relay_send, relay_recv, pass_send, pass_recv,
):
    tile = lax.axis_index("tile")
    section = lax.axis_index("section")
    half = sections // 2
    side = states.shape[1]
    rows = states.shape[2]
    chan = states.shape[3]
    received = (received_a, received_b)

    def tile_at(by):
        return lax.rem(tile + by, tiles)

    partner = tile + 1 - 2 * lax.rem(tile, 2)
    barrier = pltpu.get_barrier_semaphore()
    for by in range(1, tiles):
        pl.semaphore_signal(barrier, inc=1, device_id={"tile": tile_at(by)}, device_id_type=MESH)
    for by in range(1, sections):
        pl.semaphore_signal(
            barrier, inc=1, device_id={"section": lax.rem(section + by, sections)}, device_id_type=MESH
        )
        pl.semaphore_signal(
            barrier, inc=1, device_id={"tile": partner, "section": lax.rem(section + by, sections)},
            device_id_type=MESH,
        )
    pl.semaphore_wait(barrier, tiles - 1 + 2 * (sections - 1))

    group = sections // micro
    works = lax.rem(section, group) == 0
    mine = section // group
    my_block = placement[tile]
    sources = tiles * tiles * slots + my_block * (4 * patches)
    places = sources + tiles * 4 * patches

    @pl.loop(0, tiles)
    def _(block):
        def one(by, found):
            here = placement[lax.rem(tile - by + tiles, tiles)]
            return jnp.where(here == block, by, found)

        behind[block] = lax.fori_loop(0, tiles, one, jnp.int32(0))

    nothing = jnp.zeros((rows, 3 * chan), jnp.bfloat16)
    padded[0] = nothing
    padded[side + 1] = nothing

    column = lax.broadcasted_iota(jnp.int32, (rows // 8, 8, chan), 1)
    first = column == 0
    last = column == 7

    def halo_copy(layer, by):
        return pltpu.make_async_remote_copy(
            src_ref=outgoing.at[layer, by - 1],
            dst_ref=received[layer].at[by - 1],
            send_sem=halo_send.at[layer, by - 1],
            recv_sem=halo_recv.at[layer, by - 1],
            device_id={"tile": tile_at(by)},
            device_id_type=MESH,
        )

    pieces = ((weights.at[0], held, 0), (weights.at[1], held, 1), (skip_w, skip_held, None), (biases, bias_held, None))

    def weight_copy(piece, source, worker):
        src, dst, layer = pieces[piece]
        return pltpu.make_async_remote_copy(
            src_ref=src,
            dst_ref=dst.at[source] if layer is None else dst.at[source, layer],
            send_sem=weight_send.at[worker, piece],
            recv_sem=weight_recv.at[source, piece],
            device_id={"section": worker * group},
            device_id_type=MESH,
        )

    def own_copy(piece):
        src, dst, layer = pieces[piece]
        return pltpu.make_async_copy(
            src, dst.at[section] if layer is None else dst.at[section, layer], own_sem.at[piece]
        )

    def out_copy(m, sec):
        return pltpu.make_async_remote_copy(
            src_ref=stage.at[half + sec], dst_ref=out.at[m],
            send_sem=out_send.at[sec], recv_sem=out_recv.at[m],
            device_id={"section": sec}, device_id_type=MESH,
        )

    def need(piece, sec):
        @pl.when(sec == section)
        def _():
            own_copy(piece).wait()

        near = sec // group == mine

        @pl.when((sec != section) & (near if piece < 2 else True))
        def _():
            weight_copy(piece, sec, 0).wait_recv()

        if piece < 2:
            @pl.when(jnp.logical_not(near))
            def _():
                for hop in range(2):
                    pass_copy(piece, sec, hop, hop).wait_recv()

    deep = 3 * chan // 2

    def part(other):
        which = lax.rem(tile + other, 2)
        return pl.ds(pl.multiple_of(which * deep, LANES), deep)

    def relay_copy(layer, source, worker):
        return pltpu.make_async_remote_copy(
            src_ref=weights.at[layer, :, part(0)], dst_ref=held.at[source, layer, :, part(0)],
            send_sem=relay_send.at[worker, layer], recv_sem=relay_recv.at[source, layer],
            device_id={"section": worker * group + 1}, device_id_type=MESH,
        )

    def pass_copy(layer, source, hop, other):
        place = held.at[source, layer, :, part(other)]
        device = {"section": mine * group}
        if hop == 1:
            device["tile"] = partner
        return pltpu.make_async_remote_copy(
            src_ref=place, dst_ref=place,
            send_sem=pass_send.at[source, layer, hop], recv_sem=pass_recv.at[source, layer, hop],
            device_id=device, device_id_type=MESH,
        )

    def gelu(z):
        return 0.5 * z * (1.0 + lax.erf(z * np.float32(0.5 ** 0.5)))

    def shifted(values):
        cells = values.reshape(rows // 8, 8, chan)
        lower = jnp.where(first, 0.0, pltpu.roll(cells, 1, 1)).reshape(rows, chan)
        upper = jnp.where(last, 0.0, pltpu.roll(cells, 7, 1)).reshape(rows, chan)
        return jnp.concatenate([lower, values, upper], axis=1).astype(jnp.bfloat16)

    def run_layer(sec, layer):
        for p in range(patches):
            top = (side - 1) * rows + p * 8
            for b in range(chan // LANES):
                lanes = slice(b * LANES, (b + 1) * LANES)
                rims[4 * p, :, lanes] = hidden[b, pl.ds(p * 8, 8, stride=rows), :]
                rims[4 * p + 1, :, lanes] = hidden[b, pl.ds(p * 8 + 7, 8, stride=rows), :]
                rims[4 * p + 2, :, lanes] = hidden[b, p * 8:p * 8 + 8, :]
                rims[4 * p + 3, :, lanes] = hidden[b, top:top + 8, :]
        for by in range(1, tiles):
            base = (my_block * tiles + placement[tile_at(by)]) * slots
            for q in range(slots):
                outgoing[layer, by - 1, q] = rims[table[base + q]].astype(jnp.bfloat16)
            halo_copy(layer, by).start()

        for r in range(side):
            values = joined(hidden, slice(r * rows, (r + 1) * rows))
            padded[r + 1] = shifted(values)

        step = 2
        if layer == 0:
            need(3, sec)
            need(2, sec)
        need(layer, sec)
        @pl.loop(0, side // step)
        def _(part):
            r = part * step
            total = jnp.broadcast_to(bias_held[sec, layer:layer + 1, :], (step * rows, chan))
            for i in range(3):
                total += jnp.dot(
                    padded[pl.ds(r + i, step)].reshape(step * rows, 3 * chan),
                    held[sec, layer, i],
                    preferred_element_type=jnp.float32,
                )
            if layer == 0:
                total += jnp.dot(
                    stage[sec, pl.ds(r, step)].reshape(step * rows, chan),
                    skip_held[sec],
                    preferred_element_type=jnp.float32,
                )
            span = pl.ds(pl.multiple_of(r * rows, 8), step * rows)
            split_store(summed, span, total)
            split_store(hidden, span, gelu(total))

        for by in range(1, tiles):
            halo_copy(layer, by).wait_recv()
        for e in range(4 * patches):
            by = behind[table[sources + e]]
            row = table[places + e]
            edges[e % 4, e // 4 * 8:e // 4 * 8 + 8, :] = jnp.where(
                by == 0,
                rims[row],
                received[layer][jnp.maximum(by - 1, 0), lax.rem(row, slots)].astype(jnp.float32),
            )
        for k in (2, 3):
            row = 0 if k == 2 else side - 1
            added = jnp.dot(
                shifted(edges[k]), held[sec, layer, k * 2 - 4], preferred_element_type=jnp.float32
            )
            span = slice(row * rows, (row + 1) * rows)
            total = joined(summed, span) + added
            split_store(summed, span, total)
            split_store(hidden, span, gelu(total))
        for k in (0, 1):
            moved = shifted(edges[k])
            added = jnp.zeros((rows, chan), jnp.float32)
            for i in range(3):
                added += jnp.dot(
                    moved[:, i * chan:(i + 1) * chan],
                    held[sec, layer, i, k * 2 * chan:(k * 2 + 1) * chan],
                    preferred_element_type=jnp.float32,
                )
            for p in range(patches):
                span = pl.ds(p * 8 + k * 7, 8, stride=rows)
                for b in range(chan // LANES):
                    part = added[p * 8:p * 8 + 8, b * LANES:(b + 1) * LANES]
                    hidden[b, span, :] = gelu(summed[b, span, :] + part)
        if layer == LAYERS - 1:
            for r in range(side):
                stage[half + sec, r] = joined(hidden, slice(r * rows, (r + 1) * rows)).astype(jnp.bfloat16)
        for by in range(1, tiles):
            halo_copy(layer, by).wait_send()

    def send_weights(worker, which):
        for piece in which:
            weight_copy(piece, section, worker).start()

    @pl.when(works)
    def _():
        for piece in (3, 2, 0, 1):
            own_copy(piece).start()

    for worker in range(micro):
        @pl.when(section != worker * group)
        def _():
            send_weights(worker, (3, 2))

        @pl.when((section != worker * group) & (mine == worker))
        def _():
            send_weights(worker, (0, 1))

        @pl.when(works & (mine != worker))
        def _():
            relay_copy(0, section, worker).start()

    for worker in range(micro):
        @pl.when(works & (mine != worker))
        def _():
            for layer in range(1, LAYERS):
                relay_copy(layer - 1, section, worker).wait_send()
                relay_copy(layer, section, worker).start()

    relays = lax.rem(section, group) == 1

    def pass_on(source):
        for layer in range(LAYERS):
            relay_copy(layer, source, 0).wait_recv()
            for hop in range(2):
                pass_copy(layer, source, hop, 0).start()

    for rank in range(group):
        for worker in range(micro):
            source = worker * group + rank

            @pl.when(relays & (mine != worker))
            def _():
                pass_on(source)

        if rank + 1 < group:
            for worker in range(micro):
                @pl.when(relays & (mine != worker))
                def _():
                    pl.semaphore_signal(
                        ready.at[mine], inc=1, device_id={"section": worker * group + rank + 1},
                        device_id_type=MESH,
                    )

            for worker in range(micro):
                @pl.when((lax.rem(section, group) == rank + 1) & (mine != worker))
                def _():
                    pl.semaphore_wait(ready.at[worker], 1)
                    relay_copy(0, section, worker).start()
                    for layer in range(1, LAYERS):
                        relay_copy(layer - 1, section, worker).wait_send()
                        relay_copy(layer, section, worker).start()

    @pl.when(works)
    def _():
        for i in range(half):
            stage[i] = states[mine]
        for r in range(side):
            split_store(hidden, slice(r * rows, (r + 1) * rows), states[mine, r].astype(jnp.float32))

        @pl.loop(0, sections)
        def _(sec):
            for layer in range(LAYERS):
                run_layer(sec, layer)

            @pl.when(sec == section)
            def _():
                out[mine] = stage[half + sec]

            @pl.when(sec != section)
            def _():
                out_copy(mine, sec).start()

        @pl.loop(0, sections)
        def _(sec):
            @pl.when(sec != section)
            def _():
                out_copy(mine, sec).wait_send()

    for worker in range(micro):
        @pl.when(section != worker * group)
        def _():
            for piece in (2, 3):
                weight_copy(piece, section, worker).wait_send()
            out_copy(worker, section).wait_recv()

        @pl.when((section != worker * group) & (mine == worker))
        def _():
            for piece in (0, 1):
                weight_copy(piece, section, worker).wait_send()

        @pl.when(mine != worker)
        def _():
            relay_copy(LAYERS - 1, section, worker).wait_send()

        @pl.when(relays & (mine != worker))
        def _():
            for rank in range(group):
                for layer in range(LAYERS):
                    for hop in range(2):
                        pass_copy(layer, worker * group + rank, hop, 0).wait_send()


def on_device(states, conv_weight, skip_weight, bias, placement):
    sections = lax.axis_size("section")
    tiles = lax.axis_size("tile")
    micro, patches, side, _, chan = states.shape
    neighbour, rim_side, flip_flag = seam_tables(PR)
    assert not flip_flag.any()
    send_row, _, recv_dev, recv_slot = off_device_routes(neighbour, rim_side, flip_flag, tiles, patches)
    slots = send_row.shape[2]
    whole = patches + patches % 2
    rows = whole * side
    table = np.concatenate([x.reshape(-1) for x in (send_row, recv_dev, recv_slot)])
    ordered = states.transpose(0, 2, 1, 3, 4)
    if whole != patches:
        ordered = jnp.pad(ordered, ((0, 0), (0, 0), (0, whole - patches), (0, 0), (0, 0)))
    ordered = ordered.reshape(micro, side, rows, chan)
    weights = conv_weight[0].reshape(LAYERS, 3, 3 * chan, chan)
    biases = jnp.pad(bias[0].astype(jnp.float32), ((0, 8 - LAYERS), (0, 0)))
    held = sections + sections // 2
    smem = pl.BlockSpec(memory_space=pltpu.SMEM)
    vmem = pl.BlockSpec(memory_space=pltpu.VMEM)
    wide = pltpu.VMEM((chan // LANES, side * rows, LANES), jnp.float32)
    got = pltpu.VMEM((tiles - 1, slots, side, chan), jnp.bfloat16)
    flops = 2 * micro * side * rows * chan * chan * (9 * LAYERS + 1)
    result = pl.pallas_call(
        functools.partial(window_kernel, tiles, sections, patches, micro, slots),
        out_shape=jax.ShapeDtypeStruct((micro, side, rows, chan), jnp.bfloat16),
        in_specs=[smem] * 2 + [vmem, pl.BlockSpec(memory_space=pl.ANY), vmem, vmem],
        out_specs=vmem,
        scratch_shapes=[
            pltpu.VMEM((sections,) + weights.shape, jnp.bfloat16),
            pltpu.VMEM((sections, chan, chan), jnp.bfloat16),
            pltpu.VMEM((sections, 8, chan), jnp.float32),
            pltpu.VMEM((held, side, rows, chan), jnp.bfloat16),
            wide, wide,
            pltpu.VMEM((side + 2, rows, 3 * chan), jnp.bfloat16),
            pltpu.VMEM((4, rows, chan), jnp.float32),
            pltpu.VMEM((patches * 4, side, chan), jnp.float32),
            pltpu.VMEM((2, tiles - 1, slots, side, chan), jnp.bfloat16),
            got, got,
            pltpu.SMEM((tiles,), jnp.int32),
            pltpu.SemaphoreType.DMA((2, tiles - 1)),
            pltpu.SemaphoreType.DMA((2, tiles - 1)),
            pltpu.SemaphoreType.DMA((micro, 4)),
            pltpu.SemaphoreType.DMA((sections, 4)),
            pltpu.SemaphoreType.DMA((4,)),
            pltpu.SemaphoreType.DMA((sections,)),
            pltpu.SemaphoreType.DMA((micro,)),
            pltpu.SemaphoreType.REGULAR((micro,)),
            pltpu.SemaphoreType.DMA((micro, LAYERS)),
            pltpu.SemaphoreType.DMA((sections, LAYERS)),
            pltpu.SemaphoreType.DMA((sections, LAYERS, 2)),
            pltpu.SemaphoreType.DMA((sections, LAYERS, 2)),
        ],
        compiler_params=pltpu.CompilerParams(
            collective_id=0, has_side_effects=True, vmem_limit_bytes=56 * 1024 * 1024
        ),
        cost_estimate=pl.CostEstimate(flops=flops, bytes_accessed=2**24, transcendentals=0),
    )(
        placement, jnp.asarray(table, jnp.int32),
        ordered, weights, skip_weight[0], biases,
    )
    result = result.reshape(micro, side, whole, side, chan)[:, :, :patches]
    return result.transpose(0, 2, 1, 3, 4)[None]


def solution(mesh):
    in_specs = (
        P(None, "tile", None, None, None),
        P("section", None, None, None, None, None),
        P("section", None, None),
        P("section", None, None),
        P(),
    )
    out_specs = P("section", None, "tile", None, None, None)
    return jax.shard_map(
        on_device, mesh=mesh, in_specs=in_specs, out_specs=out_specs, check_vma=False
    )
```
